32 devices in a mesh: ia: 16 (over z, x, core), jb: 2 (over y).
Axes of the slice: x: 2, y: 2, z: 4, core: 2. Of those that a mesh axis runs over, the one named last changes fastest.
Arguments:
- density: bfloat16 [8000, 100000], P('ia', 'jb'), may hold values from -6 to 6
- chol_vectors: bfloat16 [100000, 32], P('jb', 'ia'), may hold values from -0.01953125 to 0.01953125
- virt_coef: bfloat16 [1000, 1100], P('jb'), may hold values from -0.1875 to 0.1875
Outputs:
- half_back: float32 [8, 32, 1100], P(None, ('ia', 'jb'))
The draws below stay inside these ranges and needn't reach their ends.
All inputs are finite; a program needn't handle non-finite values.
Results may differ from the reference program's by a relative error of at most 0.0003.
Values may be sent and summed in bfloat16 or wider, within the bound.
A program may use at most 128 MiB of HBM per device.

```python
import jax
import jax.numpy as jnp
from jax import lax

NOCC = 100
NV = 1000
NAO = 1100
OSLAB = 8
NCHOL = 32


def level_of(rng, extent, cuts, smallest, high):
    level, own = 1.0, jax.random.fold_in(rng, 6)
    for dim, shards_of in cuts:
        heights = jnp.exp(jax.random.uniform(jax.random.fold_in(own, dim), (shards_of,), jnp.float32, smallest / len(cuts), high / len(cuts)))
        level = level * jnp.repeat(heights, extent[dim] // shards_of).reshape([-1 if axis == dim else 1 for axis in range(len(extent))])
    return level


def noise(stream_key, shape, scale, most, cuts=(), dtype=jnp.bfloat16):
    entries = jax.random.normal(stream_key, shape, jnp.float32) * scale
    if len(cuts) > 0:
        entries = level_of(stream_key, shape, cuts, -0.22, 0.18) * entries
    return jnp.clip(entries, min=-most, max=most).astype(dtype)


def setup_inputs(seed: int = 0) -> dict:
    keys = jax.random.split(jax.random.key(seed), 4)
    return {
        "density": noise(keys[0], (OSLAB * NV, NOCC * NV), 1.0, 6.0, ((0, 16), (1, 2))),
        "chol_vectors": noise(keys[1], (NOCC * NV, NCHOL), (NOCC * NV) ** -0.5, 0.01953125, ((0, 2), (1, 16))),
        "virt_coef": noise(keys[2], (NV, NAO), NV ** -0.5, 0.1875, ((0, 2),)),
    }


def reference(density, chol_vectors, virt_coef):
    gamma_full = jnp.dot(density, chol_vectors, preferred_element_type=jnp.float32)
    gamma_full = gamma_full.reshape(OSLAB, NV, NCHOL)
    return jnp.einsum("iap,an->ipn", gamma_full, virt_coef.astype(jnp.float32), precision=lax.Precision.HIGHEST)
```

```python
import functools

import jax
import jax.numpy as jnp
from jax import lax
from jax.experimental import pallas as pl
from jax.experimental.pallas import tpu as pltpu
from jax.sharding import PartitionSpec as P

MESH = pl.DeviceIdType.MESH
LANES = 128
VMEM_BYTES = 67043328
MOST_CHUNKS = 15
AHEAD = 6
NT = (((1,), (1,)), ((), ()))


def from_root(value, axis, source):
    kept = jnp.where(lax.axis_index(axis) == source, value, 0).astype(value.dtype)
    return lax.psum(kept, axis)


def by_collectives(density, chol_vectors, virt_coef):
    row_count = density.shape[0]
    groups = lax.axis_size("jb")
    slab_devices = lax.axis_size("ia")
    all_vectors = lax.all_gather(chol_vectors, "ia", axis=1, tiled=True)
    gamma_part = jnp.dot(density, all_vectors, preferred_element_type=jnp.float32)
    owner_row = lax.axis_index("ia") % groups
    coef_block = from_root(virt_coef, "jb", owner_row).astype(jnp.float32)
    chol_count = gamma_part.shape[1]
    group_width = chol_count // slab_devices
    reduced = lax.psum_scatter(
        gamma_part.reshape(row_count, slab_devices, group_width),
        "jb",
        scatter_dimension=2,
        tiled=True,
    )
    summed = jnp.einsum("arq,an->rqn", reduced, coef_block, precision=lax.Precision.HIGHEST)
    regrouped = lax.all_to_all(summed, "ia", split_axis=0, concat_axis=0, tiled=True)
    occ_slab = slab_devices // groups
    return jnp.sum(
        regrouped.reshape(occ_slab, groups, regrouped.shape[1], regrouped.shape[2]), axis=1
    )


def chunks_of(columns):
    tiles = columns // LANES
    count = max((c for c in range(1, MOST_CHUNKS + 1) if tiles % c == 0), default=1)
    return count, tiles // count * LANES, columns - tiles * LANES


def kernel(
    slab, groups, d_hbm, v_hbm, c_hbm, o_ref,
    dbuf, vbuf, cbuf, acc, gsend, grecv,
    dsem, tsem, lsem, zs, zr, xs, xr, ks, kr, cs, cr, gs, gr,
):
    width, columns = v_hbm.shape
    count, chunk, tail = chunks_of(columns)
    last = count - 1
    line = slab // 4
    total = slab * groups
    occ = slab // groups
    r, g = lax.axis_index("ia"), lax.axis_index("jb")
    z, x, k = r // 4, (r // 2) % 2, r % 2
    linear = r * groups + g

    def device(lin):
        return (lin // groups, lin % groups)

    def place(rr):
        return ((rr % 2) * 2 + (rr // 2) % 2) * line + rr // 4

    def cols(j):
        if isinstance(j, int) and j == last:
            return pl.ds(last * chunk, chunk + tail)
        return pl.ds(pl.multiple_of(j * chunk, LANES), chunk)

    def rows(start, size):
        return pl.ds(pl.multiple_of(start * width, width), size * width)

    def d_copy(j):
        part = pl.ds(pl.multiple_of(j * chunk, LANES), chunk)
        return pltpu.make_async_copy(d_hbm.at[:, part], dbuf.at[:, part], dsem.at[j])

    rest = pl.ds(count * chunk, tail)
    d_tail = pltpu.make_async_copy(d_hbm.at[:, rest], dbuf.at[:, rest], tsem) if tail else None
    own_rows = rows(place(r), 1)
    v_local = pltpu.make_async_copy(v_hbm, vbuf.at[own_rows, :], lsem.at[0])
    c_local = pltpu.make_async_copy(c_hbm, cbuf.at[g], lsem.at[1])

    def z_copy(j, step):
        target = ((z + step) % line * 2 + x) * 2 + k
        return pltpu.make_async_remote_copy(
            v_hbm.at[:, cols(j)], vbuf.at[own_rows, cols(j)],
            zs.at[j, step - 1], zr.at[j, step - 1], device_id=(target, g), device_id_type=MESH,
        )

    def x_copy(j):
        part = vbuf.at[rows((k * 2 + x) * line, line), cols(j)]
        target = (z * 2 + 1 - x) * 2 + k
        return pltpu.make_async_remote_copy(
            part, part, xs.at[j], xr.at[j], device_id=(target, g), device_id_type=MESH
        )

    def k_copy(j):
        part = vbuf.at[rows(k * 2 * line, 2 * line), cols(j)]
        target = (z * 2 + x) * 2 + 1 - k
        return pltpu.make_async_remote_copy(
            part, part, ks.at[j], kr.at[j], device_id=(target, g), device_id_type=MESH
        )

    c_copy = pltpu.make_async_remote_copy(
        c_hbm, cbuf.at[g], cs, cr, device_id=(r, 1 - g), device_id_type=MESH
    )

    ahead = min(AHEAD, count)
    for j in range(ahead):
        d_copy(j).start()
    if tail:
        d_tail.start()
    v_local.start()
    c_local.start()

    barrier = pltpu.get_barrier_semaphore()

    def greet(step, carry):
        pl.semaphore_signal(
            barrier, inc=1, device_id=device((linear + step) % total), device_id_type=MESH
        )
        return carry

    lax.fori_loop(1, total, greet, 0)
    pl.semaphore_wait(barrier, total - 1)

    def z_send(j):
        for step in range(1, line):
            z_copy(j, step).start()

    def z_relay(j):
        for step in range(1, line):
            z_copy(j, step).wait_recv()
        x_copy(j).start()

    def x_relay(j):
        x_copy(j).wait_recv()
        k_copy(j).start()

    def multiply(j):
        k_copy(j).wait_recv()
        d_copy(j).wait()
        if tail and isinstance(j, int) and j == last:
            d_tail.wait()
        acc[...] += lax.dot_general(
            vbuf[:, cols(j)], dbuf[:, cols(j)], NT, preferred_element_type=jnp.float32
        )

    def looped(f, start, stop):
        def body(j, carry):
            f(j)
            return carry

        lax.fori_loop(start, stop, body, 0)

    looped(z_send, 0, last)
    z_send(last)
    c_copy.start()
    acc[...] = jnp.zeros_like(acc)
    v_local.wait()
    z_relay(0)
    z_relay(1)
    x_relay(0)

    def step_of(j):
        z_relay(j + 2)
        x_relay(j + 1)

        @pl.when(j + ahead < count)
        def _():
            d_copy(j + ahead).start()

        multiply(j)

    looped(step_of, 0, count - 3)
    z_relay(last)
    x_relay(last - 1)
    multiply(count - 3)
    x_relay(last)
    multiply(count - 2)
    multiply(last)

    gsend[:, 0, :] = acc[...]

    def g_copy(step):
        target = (linear + step) % total
        tr, tg = device(target)
        return pltpu.make_async_remote_copy(
            gsend.at[place(tr) * width + tg], grecv.at[g, r % groups, r // groups],
            gs.at[step], gr.at[step], device_id=(tr, tg), device_id_type=MESH,
        )

    looped(lambda step: g_copy(step).start(), 1, total)
    g_local = pltpu.make_async_copy(
        gsend.at[place(r) * width + g], grecv.at[g, r % groups, r // groups], lsem.at[2]
    )
    g_local.start()

    def sent(j):
        for step in range(1, line):
            z_copy(j, step).wait_send()
        x_copy(j).wait_send()
        k_copy(j).wait_send()

    looped(sent, 0, last)
    sent(last)
    c_local.wait()
    c_copy.wait()
    g_local.wait()
    looped(lambda step: g_copy(step).wait_recv(), 1, total)

    total_out = None
    for half in range(groups):
        gam = sum(grecv[src, half, :, 0, :] for src in range(1, groups)) + grecv[0, half, :, 0, :]
        high = gam.astype(jnp.bfloat16).astype(jnp.float32)
        left = gam - high
        mid = left.astype(jnp.bfloat16).astype(jnp.float32)
        low = left - mid
        stacked = jnp.concatenate([high, mid, low], axis=0).astype(jnp.bfloat16)
        part = lax.dot_general(stacked, cbuf[half], NT, preferred_element_type=jnp.float32)
        total_out = part if total_out is None else total_out + part
    o_ref[...] = total_out[2 * occ:] + total_out[occ:2 * occ] + total_out[:occ]
    looped(lambda step: g_copy(step).wait_send(), 1, total)


def fused(slab, groups, density, chol_vectors, virt_coef):
    rows, columns = density.shape
    width = chol_vectors.shape[1]
    coef_rows, orbitals = virt_coef.shape
    count = chunks_of(columns)[0]
    line, total, occ = slab // 4, slab * groups, slab // groups
    dma = pltpu.SemaphoreType.DMA
    out = pl.pallas_call(
        functools.partial(kernel, slab, groups),
        out_shape=jax.ShapeDtypeStruct((occ, orbitals), jnp.float32),
        in_specs=[pl.BlockSpec(memory_space=pl.ANY)] * 3,
        out_specs=pl.BlockSpec(memory_space=pltpu.VMEM),
        scratch_shapes=[
            pltpu.VMEM((rows, columns), density.dtype),
            pltpu.VMEM((slab * width, columns), chol_vectors.dtype),
            pltpu.VMEM((groups, orbitals, coef_rows), virt_coef.dtype),
            pltpu.VMEM((slab * width, rows), jnp.float32),
            pltpu.VMEM((slab * width, 1, rows), jnp.float32),
            pltpu.VMEM((groups, groups, occ, 1, rows), jnp.float32),
            dma((count,)), dma, dma((3,)),
            dma((count, line - 1)), dma((count, line - 1)),
            dma((count,)), dma((count,)), dma((count,)), dma((count,)),
            dma, dma, dma((total,)), dma((total,)),
        ],
        compiler_params=pltpu.CompilerParams(
            collective_id=0, has_side_effects=True, vmem_limit_bytes=VMEM_BYTES
        ),
    )(density, chol_vectors.T, virt_coef.T)
    return out.reshape(occ, 1, orbitals)


def on_device(slab, groups, density, chol_vectors, virt_coef):
    rows, columns = density.shape
    width = chol_vectors.shape[1]
    padded = (columns + LANES) * (rows + 16 + slab * width) * 2
    fits = padded + 8 * virt_coef.size < VMEM_BYTES - (6 << 20)
    paired = groups == 2 and width == groups and slab % 8 == 0
    if fits and paired and rows == virt_coef.shape[0] and chunks_of(columns)[0] >= 4:
        return fused(slab, groups, density, chol_vectors, virt_coef)
    return by_collectives(density, chol_vectors, virt_coef)


def solution(mesh):
    in_specs = (P("ia", "jb"), P("jb", "ia"), P("jb", None))
    out_specs = P(None, ("ia", "jb"), None)
    body = functools.partial(on_device, mesh.shape["ia"], mesh.shape["jb"])
    return jax.shard_map(body, mesh=mesh, in_specs=in_specs, out_specs=out_specs, check_vma=False)
```

```python
import functools

import jax
import jax.numpy as jnp
from jax import lax
from jax.experimental import pallas as pl
from jax.experimental.pallas import tpu as pltpu
from jax.sharding import PartitionSpec as P

MESH = pl.DeviceIdType.MESH
LANES = 128
VMEM_BYTES = 67043328
MOST_CHUNKS = 15
AHEAD = 6
LAG = 3
NT = (((1,), (1,)), ((), ()))


def from_root(value, axis, source):
    kept = jnp.where(lax.axis_index(axis) == source, value, 0).astype(value.dtype)
    return lax.psum(kept, axis)


def by_collectives(density, chol_vectors, virt_coef):
    row_count = density.shape[0]
    groups = lax.axis_size("jb")
    slab_devices = lax.axis_size("ia")
    all_vectors = lax.all_gather(chol_vectors, "ia", axis=1, tiled=True)
    gamma_part = jnp.dot(density, all_vectors, preferred_element_type=jnp.float32)
    owner_row = lax.axis_index("ia") % groups
    coef_block = from_root(virt_coef, "jb", owner_row).astype(jnp.float32)
    chol_count = gamma_part.shape[1]
    group_width = chol_count // slab_devices
    reduced = lax.psum_scatter(
        gamma_part.reshape(row_count, slab_devices, group_width),
        "jb",
        scatter_dimension=2,
        tiled=True,
    )
    summed = jnp.einsum("arq,an->rqn", reduced, coef_block, precision=lax.Precision.HIGHEST)
    regrouped = lax.all_to_all(summed, "ia", split_axis=0, concat_axis=0, tiled=True)
    occ_slab = slab_devices // groups
    return jnp.sum(
        regrouped.reshape(occ_slab, groups, regrouped.shape[1], regrouped.shape[2]), axis=1
    )


def chunks_of(columns):
    tiles = columns // LANES
    count = max((c for c in range(1, MOST_CHUNKS + 1) if tiles % c == 0), default=1)
    return count, tiles // count * LANES, columns - tiles * LANES


def kernel(
    slab, groups, d_hbm, v_hbm, c_hbm, o_ref,
    dbuf, vbuf, cbuf, acc, gsend, grecv,
    dsem, tsem, lsem, zs, zr, xs, xr, ks, kr, cs, cr, gs, gr,
):
    width, columns = v_hbm.shape
    count, chunk, tail = chunks_of(columns)
    last = count - 1
    line = slab // 4
    total = slab * groups
    occ = slab // groups
    r, g = lax.axis_index("ia"), lax.axis_index("jb")
    z, x, k = r // 4, (r // 2) % 2, r % 2
    linear = r * groups + g

    def device(lin):
        return (lin // groups, lin % groups)

    def place(rr):
        return ((rr % 2) * 2 + (rr // 2) % 2) * line + rr // 4

    def cols(j):
        if isinstance(j, int) and j == last:
            return pl.ds(last * chunk, chunk + tail)
        return pl.ds(pl.multiple_of(j * chunk, LANES), chunk)

    def rows(start, size):
        return pl.ds(pl.multiple_of(start * width, width), size * width)

    def d_copy(j):
        part = pl.ds(pl.multiple_of(j * chunk, LANES), chunk)
        return pltpu.make_async_copy(d_hbm.at[:, part], dbuf.at[:, part], dsem.at[j])

    rest = pl.ds(count * chunk, tail)
    d_tail = pltpu.make_async_copy(d_hbm.at[:, rest], dbuf.at[:, rest], tsem) if tail else None
    own_rows = rows(place(r), 1)
    v_local = pltpu.make_async_copy(v_hbm, vbuf.at[own_rows, :], lsem.at[0])
    c_local = pltpu.make_async_copy(c_hbm, cbuf.at[g], lsem.at[1])

    def z_copy(j, step):
        target = ((z + step) % line * 2 + x) * 2 + k
        return pltpu.make_async_remote_copy(
            v_hbm.at[:, cols(j)], vbuf.at[own_rows, cols(j)],
            zs.at[j, step - 1], zr.at[j, step - 1], device_id=(target, g), device_id_type=MESH,
        )

    def x_copy(j):
        part = vbuf.at[rows((k * 2 + x) * line, line), cols(j)]
        target = (z * 2 + 1 - x) * 2 + k
        return pltpu.make_async_remote_copy(
            part, part, xs.at[j], xr.at[j], device_id=(target, g), device_id_type=MESH
        )

    def k_copy(j):
        part = vbuf.at[rows(k * 2 * line, 2 * line), cols(j)]
        target = (z * 2 + x) * 2 + 1 - k
        return pltpu.make_async_remote_copy(
            part, part, ks.at[j], kr.at[j], device_id=(target, g), device_id_type=MESH
        )

    orbitals = c_hbm.shape[0]
    cut = orbitals // 32 * 16
    halves = (pl.ds(0, cut), pl.ds(cut, orbitals - cut))

    def c_over(half):
        return pltpu.make_async_remote_copy(
            c_hbm.at[halves[half], :], cbuf.at[g, halves[half], :], cs.at[0], cr.at[0],
            device_id=(r, 1 - g), device_id_type=MESH,
        )

    def c_across(half):
        part = cbuf.at[1 - g, halves[half], :]
        target = (z * 2 + x) * 2 + 1 - k
        return pltpu.make_async_remote_copy(
            part, part, cs.at[1], cr.at[1], device_id=(target, g), device_id_type=MESH
        )

    def by_core(f):
        for half in range(2):
            pl.when(k == half)(functools.partial(f, half))

    ahead = min(AHEAD, count)
    for j in range(ahead):
        d_copy(j).start()
    if tail:
        d_tail.start()
    v_local.start()
    c_local.start()

    barrier = pltpu.get_barrier_semaphore()

    def greet(step, carry):
        pl.semaphore_signal(
            barrier, inc=1, device_id=device((linear + step) % total), device_id_type=MESH
        )
        return carry

    lax.fori_loop(1, total, greet, 0)
    pl.semaphore_wait(barrier, total - 1)

    def z_send(j):
        for step in range(1, line):
            z_copy(j, step).start()

    def z_relay(j):
        for step in range(1, line):
            z_copy(j, step).wait_recv()
        x_copy(j).start()

    def x_relay(j):
        x_copy(j).wait_recv()
        k_copy(j).start()

    def multiply(j):
        k_copy(j).wait_recv()
        d_copy(j).wait()
        if tail and isinstance(j, int) and j == last:
            d_tail.wait()
        acc[...] += lax.dot_general(
            vbuf[:, cols(j)], dbuf[:, cols(j)], NT, preferred_element_type=jnp.float32
        )

    def looped(f, start, stop):
        def body(j, carry):
            f(j)
            return carry

        lax.fori_loop(start, stop, body, 0)

    looped(z_send, 0, last)
    z_send(last)
    by_core(lambda half: c_over(half).start())
    acc[...] = jnp.zeros_like(acc)
    v_local.wait()

    def step_of(t):
        fixed = isinstance(t, int)
        if not fixed or t < count:
            z_relay(t)
        if not fixed or 0 <= t - LAG < count:
            x_relay(t - LAG)
        j = t - LAG - 1
        if not fixed:
            @pl.when(j + ahead < count)
            def _():
                d_copy(j + ahead).start()
        elif 0 <= j and j + ahead < count:
            d_copy(j + ahead).start()
        if not fixed or j >= 0:
            multiply(j)

    def c_pass(half):
        c_over(half).wait_recv()
        c_across(half).start()

    for t in range(LAG + 1):
        step_of(t)
    looped(step_of, LAG + 1, last)
    step_of(last)
    by_core(c_pass)
    for t in range(count, count + LAG + 1):
        step_of(t)

    gsend[:, 0, :] = acc[...]

    def g_copy(step):
        target = (linear + step) % total
        tr, tg = device(target)
        return pltpu.make_async_remote_copy(
            gsend.at[place(tr) * width + tg], grecv.at[g, r % groups, r // groups],
            gs.at[step], gr.at[step], device_id=(tr, tg), device_id_type=MESH,
        )

    looped(lambda step: g_copy(step).start(), 1, total)
    g_local = pltpu.make_async_copy(
        gsend.at[place(r) * width + g], grecv.at[g, r % groups, r // groups], lsem.at[2]
    )
    g_local.start()

    def sent(j):
        for step in range(1, line):
            z_copy(j, step).wait_send()
        x_copy(j).wait_send()
        k_copy(j).wait_send()

    looped(sent, 0, last)
    sent(last)
    c_local.wait()

    def c_done(half):
        c_over(half).wait_send()
        c_across(half).wait_send()
        c_across(1 - half).wait_recv()

    by_core(c_done)
    g_local.wait()
    looped(lambda step: g_copy(step).wait_recv(), 1, total)

    total_out = None
    for half in range(groups):
        gam = sum(grecv[src, half, :, 0, :] for src in range(1, groups)) + grecv[0, half, :, 0, :]
        high = gam.astype(jnp.bfloat16).astype(jnp.float32)
        left = gam - high
        mid = left.astype(jnp.bfloat16).astype(jnp.float32)
        low = left - mid
        stacked = jnp.concatenate([high, mid, low], axis=0).astype(jnp.bfloat16)
        part = lax.dot_general(stacked, cbuf[half], NT, preferred_element_type=jnp.float32)
        total_out = part if total_out is None else total_out + part
    o_ref[...] = total_out[2 * occ:] + total_out[occ:2 * occ] + total_out[:occ]
    looped(lambda step: g_copy(step).wait_send(), 1, total)


def fused(slab, groups, density, chol_vectors, virt_coef):
    rows, columns = density.shape
    width = chol_vectors.shape[1]
    coef_rows, orbitals = virt_coef.shape
    count = chunks_of(columns)[0]
    line, total, occ = slab // 4, slab * groups, slab // groups
    dma = pltpu.SemaphoreType.DMA
    out = pl.pallas_call(
        functools.partial(kernel, slab, groups),
        out_shape=jax.ShapeDtypeStruct((occ, orbitals), jnp.float32),
        in_specs=[pl.BlockSpec(memory_space=pl.ANY)] * 3,
        out_specs=pl.BlockSpec(memory_space=pltpu.VMEM),
        scratch_shapes=[
            pltpu.VMEM((rows, columns), density.dtype),
            pltpu.VMEM((slab * width, columns), chol_vectors.dtype),
            pltpu.VMEM((groups, orbitals, coef_rows), virt_coef.dtype),
            pltpu.VMEM((slab * width, rows), jnp.float32),
            pltpu.VMEM((slab * width, 1, rows), jnp.float32),
            pltpu.VMEM((groups, groups, occ, 1, rows), jnp.float32),
            dma((count,)), dma, dma((3,)),
            dma((count, line - 1)), dma((count, line - 1)),
            dma((count,)), dma((count,)), dma((count,)), dma((count,)),
            dma((2,)), dma((2,)), dma((total,)), dma((total,)),
        ],
        compiler_params=pltpu.CompilerParams(
            collective_id=0, has_side_effects=True, vmem_limit_bytes=VMEM_BYTES
        ),
    )(density, chol_vectors.T, virt_coef.T)
    return out.reshape(occ, 1, orbitals)


def on_device(slab, groups, density, chol_vectors, virt_coef):
    rows, columns = density.shape
    width = chol_vectors.shape[1]
    padded = (columns + LANES) * (rows + 16 + slab * width) * 2
    fits = padded + 8 * virt_coef.size < VMEM_BYTES - (6 << 20)
    paired = groups == 2 and width == groups and slab % 8 == 0
    if fits and paired and rows == virt_coef.shape[0] and chunks_of(columns)[0] > LAG + 2:
        return fused(slab, groups, density, chol_vectors, virt_coef)
    return by_collectives(density, chol_vectors, virt_coef)


def solution(mesh):
    in_specs = (P("ia", "jb"), P("jb", "ia"), P("jb", None))
    out_specs = P(None, ("ia", "jb"), None)
    body = functools.partial(on_device, mesh.shape["ia"], mesh.shape["jb"])
    return jax.shard_map(body, mesh=mesh, in_specs=in_specs, out_specs=out_specs, check_vma=False)
```
